128 devices in a mesh: freq: 8 (over y, z_lo), rows: 16 (over z_hi, x, core).
Axes of the slice: x: 4, y: 4, z: 4 (z_hi: 2, z_lo: 2; z = z_hi * 2 + z_lo), core: 2. Of those that a mesh axis runs over, the one named last changes fastest.
Arguments:
- refl: bfloat16 [2, 16, 4608, 4608], P(None, 'freq', 'rows'), may hold values from -0.125 to 0.125
- refl_scale: float32 [16, 4608, 36], P('freq', 'rows'), may hold values from 0.5 to 4
- focus: bfloat16 [16, 4608, 128], P('freq', 'rows'), may hold values from -6 to 6
- first_mute: int32 [4608, 64], P('rows'), may hold values from 128 to 1023
- second_mute: int32 [64, 4608], P('freq', 'rows'), may hold values from 256 to 1023
Outputs:
- focus_next: float32 [64, 4608, 1024], P('freq', 'rows')
The draws below stay inside these ranges and needn't reach their ends.
All inputs are finite; a program needn't handle non-finite values.
Results may differ from the reference program's by a relative error of at most 0.0085.
Values may be sent and summed in bfloat16 or wider, within the bound.
No kernel may reach another device: no remote copies, remote signals or barrier semaphores. Data moves between devices by JAX's collectives and lax.ppermute only.
A program may use at most 128 MiB of HBM per device.

```python
import math
import jax
import jax.numpy as jnp
from jax import lax

N = 4608
P_SIZE = 64
NT = 1024
LOWBIN = 24
NF = 16
N_ROWS = 16


def set_ends(values, own_key, smallest, top_value):
    longest = values.shape.index(max(values.shape))
    spots = []
    for shift in (0, 1):
        where = [jax.random.randint(jax.random.fold_in(own_key, axis), (), 0, length) for axis, length in enumerate(values.shape)]
        where[longest] = (where[longest] + shift) % values.shape[longest]
        spots.append(tuple(where))
    return values.at[spots[0]].set(smallest).at[spots[1]].set(top_value)


def strengthened(entries, own_key, source, target, shards_of, factor):
    owner, partner = [(jnp.arange(entries.shape[dim]) // (entries.shape[dim] // shards_of)).reshape([-1 if axis == dim else 1 for axis in range(entries.ndim)]) for dim in (source, target)]
    chosen = jax.random.permutation(own_key, shards_of)[partner]
    strong = (owner == chosen) | (owner == (partner + shards_of // 2) % shards_of)
    return jnp.where(strong, factor * entries, entries)


def shard_levels(key, dims, shards, least, top_value):
    def one(dim, parts):
        heights = jax.random.uniform(jax.random.fold_in(jax.random.fold_in(key, 6), dim), (parts,), jnp.float32, least / len(shards), top_value / len(shards))
        return jnp.repeat(jnp.exp(heights), dims[dim] // parts).reshape((-1,) + (1,) * (len(dims) - dim - 1))

    gain = one(*shards[0])
    for cut in shards[1:]:
        gain = gain * one(*cut)
    return gain


def centred(key, shape, deviation, limit, pieces=(), kind=jnp.bfloat16):
    result = jax.random.normal(key, shape, jnp.float32) * deviation
    if len(pieces) > 0:
        result = shard_levels(key, shape, pieces, -0.22, 0.18) * result
    return jnp.clip(result, min=-limit, max=limit).astype(kind)


def bell_draw_with(key, shape, deviation, reach, pieces, heavy, held_as=jnp.bfloat16):
    drawn = deviation * jax.random.normal(key, shape, jnp.float32)
    if pieces:
        drawn = drawn * shard_levels(key, shape, pieces, -0.22, 0.18)
    return jnp.clip(strengthened(drawn, jax.random.fold_in(key, 3), *heavy), -reach, reach).astype(held_as)


def setup_inputs(seed: int = 0) -> dict:
    arg_keys = jax.random.split(jax.random.key(seed), 6)
    return {
        "refl": bell_draw_with(arg_keys[0], (2, NF, N, N), N ** -0.5, 0.125, ((1, 8), (2, 16)), (2, 3, 16, 2.0)),
        "refl_scale": jnp.clip(jnp.exp(math.log(4.0) - 2.0794415 * jax.random.uniform(arg_keys[1], (NF, N, N // 128), jnp.float32) ** shard_levels(arg_keys[1], (NF, N, N // 128), ((0, 8), (1, 16)), -0.2, 0.2)), 0.5, 4.0),
        "focus": centred(arg_keys[2], (NF, N, 2 * P_SIZE), 1.0, 6.0, ((0, 8), (1, 16))),
        "first_mute": set_ends(jax.random.randint(arg_keys[3], (N, P_SIZE), NT // 8, NT), jax.random.fold_in(arg_keys[3], 1), NT // 8, NT - 1).astype(jnp.int32),
        "second_mute": set_ends(jax.random.randint(arg_keys[4], (P_SIZE, N), NT // 4, NT), jax.random.fold_in(arg_keys[4], 1), NT // 4, NT - 1).astype(jnp.int32),
    }


def tables(freq_total):
    time_index = jnp.arange(NT, dtype=jnp.int32)
    freq_bins = LOWBIN + jnp.arange(freq_total, dtype=jnp.int32)
    phases = (freq_bins[:, None] * time_index[None, :] % NT).astype(jnp.float32) * (2.0 * math.pi / NT)
    inward = 1.0 / math.sqrt(2.0 * freq_total)
    outward = 2.0 / (NT * inward)
    basis_rows = jnp.concatenate([jnp.cos(phases), -jnp.sin(phases)], 0)
    return (basis_rows.T * inward, basis_rows * outward)

def decode(quantized, block_scale):
    blocks = block_scale.shape[-1]
    reshaped = quantized.reshape(quantized.shape[:3] + (blocks, quantized.shape[3] // blocks))
    return (reshaped * block_scale[None, :, :, :, None]).astype(jnp.bfloat16).reshape(quantized.shape)

def combine_first(direct, crossed, points):
    return jnp.concatenate([direct[..., :points] - crossed[..., points:], direct[..., points:] + crossed[..., :points]], -1)

def combine_second(direct, crossed, points):
    return jnp.concatenate([direct[..., :points] + crossed[..., points:], direct[..., points:] - crossed[..., :points]], -1)

def mute_pass(samples, cutoff, inverse, forward):
    traces = jnp.dot(inverse, samples.astype(jnp.float32), precision=lax.Precision.HIGHEST)
    time_index = jnp.arange(NT, dtype=jnp.int32)
    kept = jnp.where(time_index[:, None] < cutoff[None, :], traces, 0.0)
    return jnp.dot(forward, kept, precision=lax.Precision.HIGHEST).astype(jnp.bfloat16)

def reference(refl, refl_scale, focus, first_mute, second_mute):
    rows_dev = N // N_ROWS
    inverse, forward = tables(NF)
    time_index = jnp.arange(NT, dtype=jnp.int32)

    def decoded_at(freq_idx):
        return decode(refl[:, freq_idx][:, None], refl_scale[freq_idx][None])[:, 0]

    def first_freq(freq_idx):
        decoded = decoded_at(freq_idx)
        direct = jnp.dot(decoded[0], focus[freq_idx], preferred_element_type=jnp.float32)
        crossed = jnp.dot(decoded[1], focus[freq_idx], preferred_element_type=jnp.float32)
        return combine_first(direct, crossed, P_SIZE).astype(jnp.bfloat16)
    focused = lax.map(first_freq, jnp.arange(NF, dtype=jnp.int32))

    def mute_block(block_num):
        first_row = (block_num * rows_dev).astype(jnp.int32)
        piece_rows = lax.dynamic_slice_in_dim(focused, first_row, rows_dev, 1)
        samples = piece_rows.reshape(NF, rows_dev, 2, P_SIZE).transpose(2, 0, 1, 3).reshape(2 * NF, rows_dev * P_SIZE)
        cutoff = lax.dynamic_slice_in_dim(first_mute, first_row, rows_dev, 0).reshape(rows_dev * P_SIZE)
        spectra = mute_pass(samples, cutoff, inverse, forward)
        return spectra.reshape(2, NF, rows_dev, P_SIZE).transpose(1, 2, 0, 3).reshape(NF, rows_dev, 2 * P_SIZE)
    returned = lax.map(mute_block, jnp.arange(N_ROWS, dtype=jnp.int32))
    returned = returned.transpose(1, 0, 2, 3).reshape(NF, N, 2 * P_SIZE)

    def second_freq(freq_idx):
        decoded = decoded_at(freq_idx)
        direct = jnp.dot(decoded[0].T, returned[freq_idx], preferred_element_type=jnp.float32)
        crossed = jnp.dot(decoded[1].T, returned[freq_idx], preferred_element_type=jnp.float32)
        return combine_second(direct, crossed, P_SIZE).astype(jnp.bfloat16)
    adjoint = lax.map(second_freq, jnp.arange(NF, dtype=jnp.int32))

    def final_block(block_num):
        first_row = (block_num * rows_dev).astype(jnp.int32)
        piece_rows = lax.dynamic_slice_in_dim(adjoint, first_row, rows_dev, 1)
        samples = piece_rows.reshape(NF, rows_dev, 2, P_SIZE).transpose(3, 1, 2, 0).reshape(P_SIZE * rows_dev, 2 * NF).astype(jnp.float32)
        traces = jnp.dot(samples, inverse.T, precision=lax.Precision.HIGHEST).reshape(P_SIZE, rows_dev, NT)
        cutoff = lax.dynamic_slice_in_dim(second_mute, first_row, rows_dev, 1)
        return jnp.where(time_index[None, None, :] < cutoff[:, :, None], traces, 0.0)
    blocks_out = lax.map(final_block, jnp.arange(N_ROWS, dtype=jnp.int32))
    return blocks_out.transpose(1, 0, 2, 3).reshape(P_SIZE, N, NT)
```

```python
import math

import jax
import jax.numpy as jnp
import numpy as np
from jax import lax
from jax.experimental import pallas as pl
from jax.experimental.pallas import tpu as pltpu
from jax.sharding import Mesh
from jax.sharding import PartitionSpec as P

NT = 1024
LOWBIN = 24
FREQ = ("y", "zl")
ROWS = ("zh", "x", "c")
SWAP = ((0, 1), (1, 0))
BF = jnp.bfloat16
F32 = jnp.float32
MB = 1 << 20


def tables(freq_total):
    phases = (
        (LOWBIN + np.arange(freq_total))[:, None] * np.arange(NT)[None, :] % NT
    ) * (2.0 * math.pi / NT)
    inward = 1.0 / math.sqrt(2.0 * freq_total)
    outward = 2.0 / (NT * inward)
    rows = np.stack([np.cos(phases), -np.sin(phases)], 1).reshape(2 * freq_total, NT)
    return rows * inward, rows * outward


def split(table):
    upper = table.astype(BF)
    lower = (table - upper.astype(np.float64)).astype(BF)
    return upper, lower


def constants(freq_total, group):
    inverse, forward = tables(freq_total)
    rows = 2 * freq_total
    upper, lower = split(inverse)
    pair = np.concatenate([upper, lower], 0)
    zero = np.zeros_like(pair)
    inv = np.stack([np.concatenate([pair, zero], 0), np.concatenate([zero, pair], 0)])
    spread = np.zeros((rows * group, 2 * rows * group), BF)
    for q in range(rows):
        for p in range(group):
            for h in range(2):
                spread[q * group + p, p * 2 * rows + h * rows + q] = 1
    fwd = np.zeros((NT, 128), BF)
    fwd[:, :rows] = forward.T.astype(BF)
    back = np.zeros((group, 128, rows * group), BF)
    for q in range(rows):
        for p in range(group):
            back[p, q, q * group + p] = 1
    return inv, spread, fwd, back


def decode_kernel(refl_ref, scale_ref, out_ref):
    blocks = scale_ref.shape[-1]
    for b in range(blocks):
        scale = scale_ref[0, :, b : b + 1]
        for k in range(2):
            part = refl_ref[k, 0, :, b * 128 : (b + 1) * 128].astype(F32)
            out_ref[k, 0, :, b * 128 : (b + 1) * 128] = (part * scale).astype(BF)


def decode(refl, scale):
    _, freqs, rows, cols = refl.shape
    step = 48
    return pl.pallas_call(
        decode_kernel,
        grid=(freqs, rows // step),
        in_specs=[
            pl.BlockSpec((2, 1, step, cols), lambda f, s: (0, f, s, 0)),
            pl.BlockSpec((1, step, scale.shape[-1]), lambda f, s: (f, s, 0)),
        ],
        out_specs=pl.BlockSpec((2, 1, step, cols), lambda f, s: (0, f, s, 0)),
        out_shape=jax.ShapeDtypeStruct(refl.shape, BF),
        compiler_params=pltpu.CompilerParams(vmem_limit_bytes=16 * MB),
        cost_estimate=pl.CostEstimate(
            flops=refl.size, bytes_accessed=4 * refl.size, transcendentals=0
        ),
        name="decode",
    )(refl, scale)


def first_kernel(pick_ref, dec_ref, focus_ref, *rest):
    out_ref, acc_ref = rest[-2], rest[-1]
    k = pl.program_id(0)
    rows = dec_ref.shape[2]
    part = jnp.dot(
        dec_ref[...].reshape(2 * rows, dec_ref.shape[3]),
        focus_ref[...],
        preferred_element_type=F32,
    )

    @pl.when(k == 0)
    def _():
        acc_ref[...] = part

    @pl.when(k > 0)
    def _():
        acc_ref[...] += part

    @pl.when(k == pl.num_programs(0) - 1)
    def _():
        direct = acc_ref[:rows]
        crossed = pltpu.roll(acc_ref[rows:], 64, 1)
        lane = lax.broadcasted_iota(jnp.int32, direct.shape, 1)
        both = direct + jnp.where(lane < 64, -crossed, crossed)
        turned = both.T.reshape(2, 8, 8, rows)
        out_ref[:, 0] = jnp.concatenate([turned[0], turned[1]], 1).astype(BF)


def first_product(pick, decoded, focus, partial):
    _, freqs, rows, cols = decoded.shape
    step = 1152
    extra = [] if partial is None else [partial]
    return pl.pallas_call(
        first_kernel,
        grid_spec=pltpu.PrefetchScalarGridSpec(
            num_scalar_prefetch=1,
            grid=(cols // step,),
            in_specs=[
                pl.BlockSpec((2, 1, rows, step), lambda k, pick: (0, pick[0], 0, k)),
                pl.BlockSpec((step, 128), lambda k, pick: (k, 0)),
            ]
            + [pl.BlockSpec(memory_space=pl.ANY) for _ in extra],
            out_specs=pl.BlockSpec((8, 1, 16, rows), lambda k, pick: (0, pick[0], 0, 0)),
            scratch_shapes=[pltpu.VMEM((2 * rows, 128), F32)],
        ),
        out_shape=jax.ShapeDtypeStruct((8, freqs, 16, rows), BF),
        input_output_aliases={3: 0} if extra else {},
        compiler_params=pltpu.CompilerParams(vmem_limit_bytes=16 * MB),
        cost_estimate=pl.CostEstimate(
            flops=4 * rows * cols * 128, bytes_accessed=4 * rows * cols, transcendentals=0
        ),
        name="first_product",
    )(pick, decoded, focus, *extra)


def pick_column(table, column):
    lane = lax.broadcasted_iota(jnp.int32, table.shape, 1)
    return jnp.sum(jnp.where(lane == column, table, 0.0), 1, keepdims=True)


def mute_kernel(group_ref, in_ref, cut_ref, spread_ref, inv_ref, fwd_ref, back_ref, out_ref, wide_ref, ret_ref):
    p = pl.program_id(0)
    rows = in_ref.shape[-1]

    @pl.when(p == 0)
    def _():
        turned = in_ref[...].reshape(256, rows).astype(F32).T.astype(BF)
        wide = jnp.dot(turned, spread_ref[...], preferred_element_type=F32)
        for q in range(4):
            wide_ref[q] = wide[:, q * 128 : (q + 1) * 128].astype(BF)

    traces = jnp.dot(wide_ref[p // 2], inv_ref[p % 2], preferred_element_type=F32)
    cut = pick_column(cut_ref[...].astype(F32), group_ref[0] * 8 + p).astype(jnp.int32)
    time = lax.broadcasted_iota(jnp.int32, traces.shape, 1)
    kept = jnp.where(time < cut, traces, 0.0).astype(BF)
    ret_ref[p] = jnp.dot(kept, fwd_ref[...], preferred_element_type=F32).astype(BF)

    @pl.when(p == pl.num_programs(0) - 1)
    def _():
        total = jnp.dot(ret_ref[0], back_ref[0], preferred_element_type=F32)
        for q in range(1, 8):
            total += jnp.dot(ret_ref[q], back_ref[q], preferred_element_type=F32)
        out_ref[...] = total.T.reshape(8, 2, 16, rows).astype(BF)


def whole(array):
    zeros = (0,) * array.ndim
    return pl.BlockSpec(array.shape, lambda *_: zeros)


def mute(group, samples, cut, spread, inv, fwd, back):
    rows = samples.shape[-1]
    args = (samples, cut, spread, inv, fwd, back)
    return pl.pallas_call(
        mute_kernel,
        grid_spec=pltpu.PrefetchScalarGridSpec(
            num_scalar_prefetch=1,
            grid=(8,),
            in_specs=[whole(a) for a in args],
            out_specs=pl.BlockSpec(samples.shape, lambda *_: (0, 0, 0, 0)),
            scratch_shapes=[pltpu.VMEM((4, rows, 128), BF), pltpu.VMEM((8, rows, 128), BF)],
        ),
        out_shape=jax.ShapeDtypeStruct(samples.shape, BF),
        compiler_params=pltpu.CompilerParams(vmem_limit_bytes=24 * MB),
        cost_estimate=pl.CostEstimate(
            flops=8 * rows * NT * 512, bytes_accessed=4 * MB, transcendentals=0
        ),
        name="mute",
    )(group, *args)


def second_kernel(core_ref, ret_ref, dec_ref, keep_ref, send_ref, lhs_ref):
    rows = dec_ref.shape[2]

    @pl.when(pl.program_id(1) == 0)
    def _():
        direct = ret_ref[...].reshape(8, 16, rows).astype(F32)
        crossed = jnp.concatenate([direct[:, 8:], -direct[:, :8]], 1)
        lhs_ref[...] = jnp.concatenate(
            [direct.reshape(128, rows), crossed.reshape(128, rows)], 1
        ).astype(BF)

    out = jnp.dot(
        lhs_ref[...],
        dec_ref[...].reshape(2 * rows, dec_ref.shape[3]),
        preferred_element_type=F32,
    )
    even = core_ref[0] == 0
    for j in range(2):
        left = out[:, 2 * j * rows : (2 * j + 1) * rows].reshape(8, 16, rows)
        right = out[:, (2 * j + 1) * rows : (2 * j + 2) * rows].reshape(8, 16, rows)
        keep_ref[:, j, 0] = jnp.where(even, left, right).astype(BF)
        send_ref[:, j, 0] = jnp.where(even, right, left).astype(BF)


def second_product(core, returned, decoded):
    _, freqs, rows, cols = decoded.shape
    step = 4 * rows
    shape = jax.ShapeDtypeStruct((8, 8, freqs, 16, rows), BF)
    spec = pl.BlockSpec((8, 2, 1, 16, rows), lambda f, k, core: (0, k, f, 0, 0))
    return pl.pallas_call(
        second_kernel,
        grid_spec=pltpu.PrefetchScalarGridSpec(
            num_scalar_prefetch=1,
            grid=(freqs, cols // step),
            in_specs=[
                pl.BlockSpec((8, 1, 16, rows), lambda f, k, core: (0, f, 0, 0)),
                pl.BlockSpec((2, 1, rows, step), lambda f, k, core: (0, f, 0, k)),
            ],
            out_specs=[spec, spec],
            scratch_shapes=[pltpu.VMEM((128, 2 * rows), BF)],
        ),
        out_shape=[shape, shape],
        compiler_params=pltpu.CompilerParams(vmem_limit_bytes=24 * MB),
        cost_estimate=pl.CostEstimate(
            flops=8 * rows * cols * 128, bytes_accessed=10 * rows * cols, transcendentals=0
        ),
        name="second_product",
    )(core, returned, decoded)


def final_kernel(in_ref, cut_ref, spread_ref, inv_ref, out_ref, wide_ref, edge_ref):
    p = pl.program_id(0)
    rows = in_ref.shape[-1]

    @pl.when(p == 0)
    def _():
        total = in_ref[:, 0].astype(F32)
        for j in range(1, 8):
            total += in_ref[:, j].astype(F32)
        turned = total.reshape(256, rows).T.astype(BF)
        wide = jnp.dot(turned, spread_ref[...], preferred_element_type=F32)
        for q in range(4):
            wide_ref[q] = wide[:, q * 128 : (q + 1) * 128].astype(BF)
        edge_ref[...] = cut_ref[...].astype(F32).T

    traces = jnp.dot(wide_ref[p // 2], inv_ref[p % 2], preferred_element_type=F32)
    cut = pick_column(edge_ref[...], p).astype(jnp.int32)
    time = lax.broadcasted_iota(jnp.int32, traces.shape, 1)
    out_ref[0] = jnp.where(time < cut, traces, 0.0)


def final(partials, cut, spread, inv):
    rows = partials.shape[-1]
    args = (partials, cut, spread, inv)
    return pl.pallas_call(
        final_kernel,
        grid=(8,),
        in_specs=[whole(a) for a in args],
        out_specs=pl.BlockSpec((1, rows, NT), lambda p: (p, 0, 0)),
        scratch_shapes=[pltpu.VMEM((4, rows, 128), BF), pltpu.VMEM((rows, 8), F32)],
        out_shape=jax.ShapeDtypeStruct((8, rows, NT), F32),
        compiler_params=pltpu.CompilerParams(vmem_limit_bytes=24 * MB),
        cost_estimate=pl.CostEstimate(
            flops=8 * rows * NT * 256, bytes_accessed=12 * MB, transcendentals=0
        ),
        name="final",
    )(*args)


def on_device(refl, refl_scale, focus, first_mute, second_mute):
    _, freqs, rows, _ = refl.shape
    core = lax.axis_index("c").astype(jnp.int32)[None]
    group = lax.axis_index(FREQ).astype(jnp.int32)[None]
    inv, spread, fwd, back = (jnp.asarray(a) for a in constants(8 * freqs, 8))

    shares = jnp.broadcast_to(focus[None], (8, 2, rows, 128)).reshape(16, rows, 128)
    own = lax.all_to_all(shares, ROWS, 0, 0, tiled=True).reshape(16 * rows, 128)
    decoded = decode(refl, refl_scale)
    other = lax.ppermute(own, "c", SWAP)
    half = first_product(core, decoded, own, None)
    focused = first_product(1 - core, decoded, other, half)
    samples = lax.all_to_all(focused, FREQ, 0, 0, tiled=True)
    spectra = mute(group, samples, first_mute, spread, inv, fwd, back)
    returned = lax.all_to_all(spectra, FREQ, 0, 0, tiled=True)
    keep, send = second_product(core, returned, decoded)
    got = lax.ppermute(send, "c", SWAP)
    summed = (keep.astype(F32) + got.astype(F32)).astype(BF)
    partials = lax.all_to_all(
        summed.reshape(64, 2 * 16, rows), FREQ + ("zh", "x"), 0, 0, tiled=True
    )
    return final(partials.reshape(8, 8, 32, rows), second_mute, spread, inv)


def solution(mesh):
    fine = Mesh(mesh.devices.reshape(4, 2, 2, 4, 2), ("y", "zl", "zh", "x", "c"))
    in_specs = (
        P(None, FREQ, ROWS, None),
        P(FREQ, ROWS, None),
        P(FREQ, ROWS, None),
        P(ROWS, None),
        P(FREQ, ROWS),
    )
    return jax.shard_map(
        on_device, mesh=fine, in_specs=in_specs, out_specs=P(FREQ, ROWS, None), check_vma=False
    )
```

```python
import functools
import math

import jax
import jax.numpy as jnp
import numpy as np
from jax import lax
from jax.experimental import pallas as pl
from jax.experimental.pallas import tpu as pltpu
from jax.sharding import Mesh
from jax.sharding import PartitionSpec as P

NT = 1024
LOWBIN = 24
FREQ = ("y", "zl")
ROWS = ("zh", "x", "c")
SWAP = ((0, 1), (1, 0))
BF = jnp.bfloat16
F32 = jnp.float32
MB = 1 << 20
VL1 = 20 * MB
VL2 = 26 * MB
KSTEP = 1152
AHEAD = 8


def tables(freq_total):
    phases = (
        (LOWBIN + np.arange(freq_total))[:, None] * np.arange(NT)[None, :] % NT
    ) * (2.0 * math.pi / NT)
    inward = 1.0 / math.sqrt(2.0 * freq_total)
    outward = 2.0 / (NT * inward)
    rows = np.stack([np.cos(phases), -np.sin(phases)], 1).reshape(2 * freq_total, NT)
    return rows * inward, rows * outward


def split(table):
    upper = table.astype(BF)
    lower = (table - upper.astype(np.float64)).astype(BF)
    return upper, lower


def constants(freq_total, group):
    inverse, forward = tables(freq_total)
    rows = 2 * freq_total
    upper, lower = split(inverse)
    pair = np.concatenate([upper, lower], 0)
    zero = np.zeros_like(pair)
    inv = np.stack([np.concatenate([pair, zero], 0), np.concatenate([zero, pair], 0)])
    spread = np.zeros((rows * group, 2 * rows * group), BF)
    for q in range(rows):
        for p in range(group):
            for h in range(2):
                spread[q * group + p, p * 2 * rows + h * rows + q] = 1
    fwd = np.zeros((NT, 128), BF)
    fwd[:, :rows] = forward.T.astype(BF)
    back = np.zeros((group, 128, rows * group), BF)
    for q in range(rows):
        for p in range(group):
            back[p, q, q * group + p] = 1
    mixed = spread.reshape(group, 2, 2, group, -1).transpose(1, 2, 0, 3, 4).reshape(spread.shape)
    return inv, spread, fwd, back, mixed


def decode_kernel(refl_ref, scale_ref, out_ref):
    blocks = scale_ref.shape[-1]
    for b in range(blocks):
        scale = scale_ref[0, :, b : b + 1]
        for k in range(2):
            part = refl_ref[k, 0, :, b * 128 : (b + 1) * 128].astype(F32)
            out_ref[k, 0, :, b * 128 : (b + 1) * 128] = (part * scale).astype(BF)


def decode(refl, scale):
    _, freqs, rows, cols = refl.shape
    step = 48
    return pl.pallas_call(
        decode_kernel,
        grid=(freqs, rows // step),
        in_specs=[
            pl.BlockSpec((2, 1, step, cols), lambda f, s: (0, f, s, 0)),
            pl.BlockSpec((1, step, scale.shape[-1]), lambda f, s: (f, s, 0)),
        ],
        out_specs=pl.BlockSpec((2, 1, step, cols), lambda f, s: (0, f, s, 0)),
        out_shape=jax.ShapeDtypeStruct(refl.shape, BF),
        compiler_params=pltpu.CompilerParams(vmem_limit_bytes=52 * MB),
        cost_estimate=pl.CostEstimate(
            flops=refl.size, bytes_accessed=4 * refl.size, transcendentals=0
        ),
        name="decode",
    )(refl, scale)


def turn(sums, rows):
    direct = sums[:rows]
    crossed = pltpu.roll(sums[rows:], 64, 1)
    lane = lax.broadcasted_iota(jnp.int32, direct.shape, 1)
    both = direct + jnp.where(lane < 64, -crossed, crossed)
    turned = both.T.reshape(2, 8, 8, rows)
    return jnp.concatenate([turned[0], turned[1]], 1).astype(BF)


def first_own_kernel(core_ref, group_ref, dec_ref, focus_ref, out_ref, own_ref, other_ref, acc_ref, sem):
    f = core_ref[0]
    _, rows, cols = own_ref.shape
    spans = [slice(k * KSTEP, (k + 1) * KSTEP) for k in range(cols // KSTEP)]
    copies = []
    for ref, which in ((own_ref, f), (other_ref, 1 - f)):
        for here in spans:
            copies.append(
                pltpu.make_async_copy(
                    dec_ref.at[:, which, :, here], ref.at[:, :, here], sem.at[len(copies)]
                )
            )
    for copy in copies[:AHEAD]:
        copy.start()
    for k, here in enumerate(spans):
        copies[k].wait()
        if k + AHEAD < len(copies):
            copies[k + AHEAD].start()
        part = jnp.dot(
            own_ref[:, :, here].reshape(2 * rows, KSTEP),
            focus_ref[here],
            preferred_element_type=F32,
        )
        if k == 0:
            acc_ref[...] = part
        else:
            acc_ref[...] += part
    for copy in copies[len(spans) + AHEAD :]:
        copy.start()
    out_ref[:, f] = turn(acc_ref[...], rows)
    for copy in copies[len(spans) :]:
        copy.wait()


def first_other_kernel(core_ref, dec_ref, focus_ref, half_ref, out_ref, acc_ref):
    f = 1 - core_ref[0]
    _, rows, cols = dec_ref.shape
    for k in range(cols // KSTEP):
        here = slice(k * KSTEP, (k + 1) * KSTEP)
        part = jnp.dot(
            dec_ref[:, :, here].reshape(2 * rows, KSTEP),
            focus_ref[here],
            preferred_element_type=F32,
        )
        if k == 0:
            acc_ref[...] = part
        else:
            acc_ref[...] += part
    out_ref[:, f] = turn(acc_ref[...], rows)
    out_ref[:, 1 - f] = half_ref[:, 1 - f]


VMEM = pl.BlockSpec(memory_space=pltpu.VMEM)
SMEM = pl.BlockSpec(memory_space=pltpu.SMEM)


def first_own(core, group, decoded, focus):
    _, freqs, rows, cols = decoded.shape
    held = jax.ShapeDtypeStruct((2, rows, cols), BF)
    return pl.pallas_call(
        first_own_kernel,
        in_specs=[SMEM, SMEM, pl.BlockSpec(memory_space=pltpu.HBM), VMEM],
        out_specs=[VMEM] * 3,
        scratch_shapes=[
            pltpu.VMEM((2 * rows, 128), F32),
            pltpu.SemaphoreType.DMA((2 * cols // KSTEP,)),
        ],
        out_shape=[jax.ShapeDtypeStruct((8, freqs, 16, rows), BF), held, held],
        compiler_params=pltpu.CompilerParams(vmem_limit_bytes=VL1),
        cost_estimate=pl.CostEstimate(
            flops=4 * rows * cols * 128, bytes_accessed=8 * rows * cols, transcendentals=0
        ),
        name="first_own",
    )(core, group, decoded, focus)


def first_other(core, held, focus, half):
    _, rows, cols = held.shape
    return pl.pallas_call(
        first_other_kernel,
        in_specs=[SMEM, VMEM, VMEM, VMEM],
        out_specs=VMEM,
        scratch_shapes=[pltpu.VMEM((2 * rows, 128), F32)],
        out_shape=jax.ShapeDtypeStruct(half.shape, BF),
        compiler_params=pltpu.CompilerParams(vmem_limit_bytes=VL1),
        cost_estimate=pl.CostEstimate(
            flops=4 * rows * cols * 128, bytes_accessed=4 * rows * cols, transcendentals=0
        ),
        name="first_other",
    )(core, held, focus, half)


def mute_kernel(group_ref, in_ref, cut_ref, spread_ref, inv_ref, fwd_ref, back_ref, out_ref, wide_ref):
    rows = in_ref.shape[-1]
    turned = in_ref[...].reshape(256, rows).astype(F32).T.astype(BF)
    wide = jnp.dot(turned, spread_ref[...], preferred_element_type=F32)
    for q in range(4):
        wide_ref[q] = wide[:, q * 128 : (q + 1) * 128].astype(BF)
    own = pl.ds(pl.multiple_of(group_ref[0] * 8, 8), 8)
    edge = cut_ref[own].astype(F32).T
    total = None
    for p in range(8):
        traces = jnp.dot(wide_ref[p // 2], inv_ref[p % 2], preferred_element_type=F32)
        cut = edge[:, p : p + 1].astype(jnp.int32)
        time = lax.broadcasted_iota(jnp.int32, traces.shape, 1)
        kept = jnp.where(time < cut, traces, 0.0).astype(BF)
        ret = jnp.dot(kept, fwd_ref[...], preferred_element_type=F32).astype(BF)
        part = jnp.dot(ret, back_ref[p], preferred_element_type=F32)
        total = part if total is None else total + part
    out_ref[...] = total.T.reshape(8, 2, 16, rows).astype(BF)


def mute(group, samples, cut, spread, inv, fwd, back):
    rows = samples.shape[-1]
    return pl.pallas_call(
        mute_kernel,
        in_specs=[SMEM] + [VMEM] * 6,
        out_specs=VMEM,
        scratch_shapes=[pltpu.VMEM((4, rows, 128), BF)],
        out_shape=jax.ShapeDtypeStruct(samples.shape, BF),
        compiler_params=pltpu.CompilerParams(vmem_limit_bytes=24 * MB),
        cost_estimate=pl.CostEstimate(
            flops=8 * rows * NT * 512, bytes_accessed=4 * MB, transcendentals=0
        ),
        name="mute",
    )(group, samples, cut, spread, inv, fwd, back)


def second_kernel(base, core_ref, ret_ref, own_ref, other_ref, keep_ref, send_ref, lhs_ref):
    rows = own_ref.shape[1]
    even = core_ref[0] == 0

    @pl.when(pl.program_id(0) == 0)
    def _():
        for f in range(2):
            direct = ret_ref[:, f].astype(F32)
            crossed = jnp.concatenate([direct[:, 8:], -direct[:, :8]], 1)
            lhs_ref[f] = jnp.concatenate(
                [direct.reshape(128, rows), crossed.reshape(128, rows)], 1
            ).astype(BF)

    parts = []
    step = 4 * rows
    here = pl.ds(pl.multiple_of((base + pl.program_id(0)) * step, 128), step)
    for k, ref in enumerate((own_ref, other_ref)):
        f = core_ref[0] if k == 0 else 1 - core_ref[0]
        parts.append(
            jnp.dot(
                lhs_ref[f],
                ref[:, :, here].reshape(2 * rows, step),
                preferred_element_type=F32,
            ).reshape(8, 2, 8, step)
        )
    parts = [
        jnp.where(even, parts[f], parts[1 - f])[:, k] for f in range(2) for k in range(2)
    ]
    lane = lax.broadcasted_iota(jnp.int32, (8, 8, 128), 2)
    low, first = lane < 64, (lane // 32) % 2 == 0
    pieces = []
    for v in range(4 * rows // 128):
        a, b, c, d = (x[:, :, v * 128 : (v + 1) * 128] for x in parts)
        a, c = jnp.where(low, a, pltpu.roll(c, 64, 2)), jnp.where(low, pltpu.roll(a, 64, 2), c)
        b, d = jnp.where(low, b, pltpu.roll(d, 64, 2)), jnp.where(low, pltpu.roll(b, 64, 2), d)
        a, b = jnp.where(first, a, pltpu.roll(b, 32, 2)), jnp.where(first, pltpu.roll(a, 96, 2), b)
        c, d = jnp.where(first, c, pltpu.roll(d, 32, 2)), jnp.where(first, pltpu.roll(c, 96, 2), d)
        pieces += [a, b, c, d]
    per = rows // 32
    for j in range(2):
        left = jnp.concatenate(pieces[2 * j * per : (2 * j + 1) * per], 1)
        right = jnp.concatenate(pieces[(2 * j + 1) * per : (2 * j + 2) * per], 1)
        keep_ref[:, j] = jnp.where(even, left, right).astype(BF)
        send_ref[:, j] = jnp.where(even, right, left).astype(BF)


def second_product(core, returned, own, other, part):
    freqs = 2
    _, rows, cols = own.shape
    step = 4 * rows
    packed = rows // 32 * 8
    shape = jax.ShapeDtypeStruct((8, 4, packed, 128), BF)
    spec = pl.BlockSpec((8, 2, packed, 128), lambda k, core: (0, k, 0, 0))
    return pl.pallas_call(
        functools.partial(second_kernel, 2 * part),
        grid_spec=pltpu.PrefetchScalarGridSpec(
            num_scalar_prefetch=1,
            grid=(cols // step // 2,),
            in_specs=[
                pl.BlockSpec((8, freqs, 16, rows), lambda k, core: (0, 0, 0, 0)),
                pl.BlockSpec(memory_space=pltpu.VMEM),
                pl.BlockSpec(memory_space=pltpu.VMEM),
            ],
            out_specs=[spec, spec],
            scratch_shapes=[pltpu.VMEM((2, 128, 2 * rows), BF)],
        ),
        out_shape=[shape, shape],
        compiler_params=pltpu.CompilerParams(vmem_limit_bytes=VL2),
        cost_estimate=pl.CostEstimate(
            flops=4 * rows * cols * 128, bytes_accessed=5 * rows * cols, transcendentals=0
        ),
        name="second_product",
    )(core, returned, own, other)


def merge_kernel(a_ref, b_ref, c_ref, d_ref, out_ref):
    for g in range(8):
        out_ref[g, :4] = (a_ref[g].astype(F32) + b_ref[g].astype(F32)).astype(BF)
        out_ref[g, 4:] = (c_ref[g].astype(F32) + d_ref[g].astype(F32)).astype(BF)


def merge(*parts):
    return pl.pallas_call(
        merge_kernel,
        in_specs=[VMEM] * 4,
        out_specs=VMEM,
        out_shape=jax.ShapeDtypeStruct((8, 8) + parts[0].shape[2:], BF),
        compiler_params=pltpu.CompilerParams(vmem_limit_bytes=8 * MB),
        name="merge",
    )(*parts)


def final_kernel(in_ref, cut_ref, spread_ref, inv_ref, out_ref, wide_ref, slab_ref, sem):
    per = in_ref.shape[2] // 8
    total = in_ref[:, 0].astype(F32)
    for j in range(1, 8):
        total += in_ref[:, j].astype(F32)
    slabs = []
    for k in range(per):
        turned = total[:, k * 8 : (k + 1) * 8].reshape(64, 128).T
        slabs.append(jnp.concatenate([turned[t * 32 : (t + 1) * 32] for t in range(4)], 1))
    turned = jnp.concatenate(slabs, 0).astype(BF)
    wide = jnp.dot(turned, spread_ref[...], preferred_element_type=F32)
    for q in range(4):
        wide_ref[q] = wide[:, q * 128 : (q + 1) * 128].astype(BF)
    edge = cut_ref[...].astype(F32).T

    def out(p):
        return pltpu.make_async_copy(slab_ref.at[p], out_ref.at[p], sem.at[p])

    for p in range(8):
        traces = jnp.dot(wide_ref[p // 2], inv_ref[p % 2], preferred_element_type=F32)
        cut = edge[:, p : p + 1].astype(jnp.int32)
        time = lax.broadcasted_iota(jnp.int32, traces.shape, 1)
        slab_ref[p] = jnp.where(time < cut, traces, 0.0)
        out(p).start()
    for p in range(8):
        out(p).wait()


def final(partials, cut, spread, inv):
    rows = cut.shape[1]
    args = (partials, cut, spread, inv)
    return pl.pallas_call(
        final_kernel,
        in_specs=[VMEM] * 4,
        out_specs=pl.BlockSpec(memory_space=pltpu.HBM),
        scratch_shapes=[
            pltpu.VMEM((4, rows, 128), BF),
            pltpu.VMEM((8, rows, NT), F32),
            pltpu.SemaphoreType.DMA((8,)),
        ],
        out_shape=jax.ShapeDtypeStruct((8, rows, NT), F32),
        compiler_params=pltpu.CompilerParams(vmem_limit_bytes=24 * MB),
        cost_estimate=pl.CostEstimate(
            flops=8 * rows * NT * 256, bytes_accessed=12 * MB, transcendentals=0
        ),
        name="final",
    )(*args)


def on_device(refl, refl_scale, focus, first_mute, second_mute):
    _, freqs, rows, _ = refl.shape
    core = lax.axis_index("c").astype(jnp.int32)[None]
    group = lax.axis_index(FREQ).astype(jnp.int32)[None]
    inv, spread, fwd, back, mixed = (jnp.asarray(a) for a in constants(8 * freqs, 8))

    shares = jnp.broadcast_to(focus[None], (8, 2, rows, 128)).reshape(16, rows, 128)
    own = lax.all_to_all(shares, ROWS, 0, 0, tiled=True).reshape(16 * rows, 128)
    decoded = pltpu.with_memory_space_constraint(decode(refl, refl_scale), pltpu.HBM)
    other = lax.ppermute(own, "c", SWAP)
    half, dec_own, dec_other = first_own(core, group, decoded, own)
    focused = first_other(core, dec_other, other, half)
    samples = lax.all_to_all(focused, FREQ, 0, 0, tiled=True)
    spectra = mute(group, samples, first_mute.T, spread, inv, fwd, back)
    returned = lax.all_to_all(spectra, FREQ, 0, 0, tiled=True)
    keep_a, send_a = second_product(core, returned, dec_own, dec_other, 0)
    got_a = lax.ppermute(send_a, "c", SWAP)
    keep_b, send_b = second_product(core, returned, dec_own, dec_other, 1)
    got_b = lax.ppermute(send_b, "c", SWAP)
    summed = merge(keep_a, got_a, keep_b, got_b)
    partials = lax.all_to_all(
        summed.reshape(64, -1, 128), FREQ + ("zh", "x"), 0, 0, tiled=True
    )
    return final(partials.reshape(8, 8, -1, 128), second_mute, mixed, inv)


def solution(mesh):
    fine = Mesh(mesh.devices.reshape(4, 2, 2, 4, 2), ("y", "zl", "zh", "x", "c"))
    in_specs = (
        P(None, FREQ, ROWS, None),
        P(FREQ, ROWS, None),
        P(FREQ, ROWS, None),
        P(ROWS, None),
        P(FREQ, ROWS),
    )
    return jax.shard_map(
        on_device, mesh=fine, in_specs=in_specs, out_specs=P(FREQ, ROWS, None), check_vma=False
    )
```

```python
import functools
import math

import jax
import jax.numpy as jnp
import numpy as np
from jax import lax
from jax.experimental import pallas as pl
from jax.experimental.pallas import tpu as pltpu
from jax.sharding import Mesh
from jax.sharding import PartitionSpec as P

NT = 1024
LOWBIN = 24
FREQ = ("y", "zl")
ROWS = ("zh", "x", "c")
SWAP = ((0, 1), (1, 0))
BF = jnp.bfloat16
F32 = jnp.float32
MB = 1 << 20
VL1 = 20 * MB
VL2 = 26 * MB
KSTEP = 1152
AHEAD = 8


def tables(freq_total):
    phases = (
        (LOWBIN + np.arange(freq_total))[:, None] * np.arange(NT)[None, :] % NT
    ) * (2.0 * math.pi / NT)
    inward = 1.0 / math.sqrt(2.0 * freq_total)
    outward = 2.0 / (NT * inward)
    rows = np.stack([np.cos(phases), -np.sin(phases)], 1).reshape(2 * freq_total, NT)
    return rows * inward, rows * outward


def split(table):
    upper = table.astype(BF)
    lower = (table - upper.astype(np.float64)).astype(BF)
    return upper, lower


def constants(freq_total, group):
    inverse, forward = tables(freq_total)
    rows = 2 * freq_total
    upper, lower = split(inverse)
    pair = np.concatenate([upper, lower], 0)
    zero = np.zeros_like(pair)
    inv = np.stack([np.concatenate([pair, zero], 0), np.concatenate([zero, pair], 0)])
    spread = np.zeros((rows * group, 2 * rows * group), BF)
    for q in range(rows):
        for p in range(group):
            for h in range(2):
                spread[q * group + p, p * 2 * rows + h * rows + q] = 1
    fwd = np.zeros((NT, 128), BF)
    fwd[:, :rows] = forward.T.astype(BF)
    back = np.zeros((group, 128, rows * group), BF)
    for q in range(rows):
        for p in range(group):
            back[p, q, q * group + p] = 1
    mixed = spread.reshape(group, 2, 2, group, -1).transpose(1, 2, 0, 3, 4).reshape(spread.shape)
    return inv, spread, fwd, back, mixed


def repeat_kernel(in_ref, out_ref, sem):
    copies = [
        pltpu.make_async_copy(in_ref, out_ref.at[k], sem.at[k]) for k in range(out_ref.shape[0])
    ]
    for copy in copies:
        copy.start()
    for copy in copies:
        copy.wait()


def repeat(array, times):
    return pl.pallas_call(
        repeat_kernel,
        in_specs=[pl.BlockSpec(memory_space=pltpu.VMEM)],
        out_specs=pl.BlockSpec(memory_space=pltpu.HBM),
        scratch_shapes=[pltpu.SemaphoreType.DMA((times,))],
        out_shape=jax.ShapeDtypeStruct((times,) + array.shape, array.dtype),
        name="repeat",
    )(array)


def decode_kernel(refl_ref, scale_ref, out_ref):
    blocks = scale_ref.shape[-1]
    for b in range(blocks):
        scale = scale_ref[0, :, b : b + 1]
        for k in range(2):
            part = refl_ref[k, 0, :, b * 128 : (b + 1) * 128].astype(F32)
            out_ref[k, 0, :, b * 128 : (b + 1) * 128] = (part * scale).astype(BF)


def decode(refl, scale):
    _, freqs, rows, cols = refl.shape
    step = rows
    return pl.pallas_call(
        decode_kernel,
        grid=(freqs, rows // step),
        in_specs=[
            pl.BlockSpec((2, 1, step, cols), lambda f, s: (0, f, s, 0)),
            pl.BlockSpec((1, step, scale.shape[-1]), lambda f, s: (f, s, 0)),
        ],
        out_specs=pl.BlockSpec((2, 1, step, cols), lambda f, s: (0, f, s, 0)),
        out_shape=jax.ShapeDtypeStruct(refl.shape, BF),
        compiler_params=pltpu.CompilerParams(vmem_limit_bytes=52 * MB),
        cost_estimate=pl.CostEstimate(
            flops=refl.size, bytes_accessed=4 * refl.size, transcendentals=0
        ),
        name="decode",
    )(refl, scale)


def turn(sums, rows):
    direct = sums[:rows]
    crossed = pltpu.roll(sums[rows:], 64, 1)
    lane = lax.broadcasted_iota(jnp.int32, direct.shape, 1)
    both = direct + jnp.where(lane < 64, -crossed, crossed)
    turned = both.T.reshape(2, 8, 8, rows)
    return jnp.concatenate([turned[0], turned[1]], 1).astype(BF)


def first_own_kernel(core_ref, group_ref, dec_ref, focus_ref, out_ref, own_ref, other_ref, acc_ref, sem):
    f = core_ref[0]
    _, rows, cols = own_ref.shape
    spans = [slice(k * KSTEP, (k + 1) * KSTEP) for k in range(cols // KSTEP)]
    copies = []
    for ref, which in ((own_ref, f), (other_ref, 1 - f)):
        for here in spans:
            copies.append(
                pltpu.make_async_copy(
                    dec_ref.at[:, which, :, here], ref.at[:, :, here], sem.at[len(copies)]
                )
            )
    for copy in copies[:AHEAD]:
        copy.start()
    for k, here in enumerate(spans):
        copies[k].wait()
        if k + AHEAD < len(copies):
            copies[k + AHEAD].start()
        part = jnp.dot(
            own_ref[:, :, here].reshape(2 * rows, KSTEP),
            focus_ref[here],
            preferred_element_type=F32,
        )
        if k == 0:
            acc_ref[...] = part
        else:
            acc_ref[...] += part
    for copy in copies[len(spans) + AHEAD :]:
        copy.start()
    out_ref[:, f] = turn(acc_ref[...], rows)
    for copy in copies[len(spans) :]:
        copy.wait()


def first_other_kernel(core_ref, dec_ref, focus_ref, half_ref, out_ref, acc_ref):
    f = 1 - core_ref[0]
    _, rows, cols = dec_ref.shape
    for k in range(cols // KSTEP):
        here = slice(k * KSTEP, (k + 1) * KSTEP)
        part = jnp.dot(
            dec_ref[:, :, here].reshape(2 * rows, KSTEP),
            focus_ref[here],
            preferred_element_type=F32,
        )
        if k == 0:
            acc_ref[...] = part
        else:
            acc_ref[...] += part
    out_ref[:, f] = turn(acc_ref[...], rows)
    out_ref[:, 1 - f] = half_ref[:, 1 - f]


VMEM = pl.BlockSpec(memory_space=pltpu.VMEM)
SMEM = pl.BlockSpec(memory_space=pltpu.SMEM)


def first_own(core, group, decoded, focus):
    _, freqs, rows, cols = decoded.shape
    held = jax.ShapeDtypeStruct((2, rows, cols), BF)
    return pl.pallas_call(
        first_own_kernel,
        in_specs=[SMEM, SMEM, pl.BlockSpec(memory_space=pltpu.HBM), VMEM],
        out_specs=[VMEM] * 3,
        scratch_shapes=[
            pltpu.VMEM((2 * rows, 128), F32),
            pltpu.SemaphoreType.DMA((2 * cols // KSTEP,)),
        ],
        out_shape=[jax.ShapeDtypeStruct((8, freqs, 16, rows), BF), held, held],
        compiler_params=pltpu.CompilerParams(vmem_limit_bytes=VL1),
        cost_estimate=pl.CostEstimate(
            flops=4 * rows * cols * 128, bytes_accessed=8 * rows * cols, transcendentals=0
        ),
        name="first_own",
    )(core, group, decoded, focus)


def first_other(core, held, focus, half):
    _, rows, cols = held.shape
    return pl.pallas_call(
        first_other_kernel,
        in_specs=[SMEM, VMEM, VMEM, VMEM],
        out_specs=VMEM,
        scratch_shapes=[pltpu.VMEM((2 * rows, 128), F32)],
        out_shape=jax.ShapeDtypeStruct(half.shape, BF),
        compiler_params=pltpu.CompilerParams(vmem_limit_bytes=VL1),
        cost_estimate=pl.CostEstimate(
            flops=4 * rows * cols * 128, bytes_accessed=4 * rows * cols, transcendentals=0
        ),
        name="first_other",
    )(core, held, focus, half)


def mute_kernel(group_ref, in_ref, cut_ref, spread_ref, inv_ref, fwd_ref, back_ref, out_ref, wide_ref):
    rows = in_ref.shape[-1]
    turned = in_ref[...].reshape(256, rows).astype(F32).T.astype(BF)
    wide = jnp.dot(turned, spread_ref[...], preferred_element_type=F32)
    for q in range(4):
        wide_ref[q] = wide[:, q * 128 : (q + 1) * 128].astype(BF)
    own = pl.ds(pl.multiple_of(group_ref[0] * 8, 8), 8)
    edge = cut_ref[own].astype(F32).T
    total = None
    for p in range(8):
        traces = jnp.dot(wide_ref[p // 2], inv_ref[p % 2], preferred_element_type=F32)
        cut = edge[:, p : p + 1].astype(jnp.int32)
        time = lax.broadcasted_iota(jnp.int32, traces.shape, 1)
        kept = jnp.where(time < cut, traces, 0.0).astype(BF)
        ret = jnp.dot(kept, fwd_ref[...], preferred_element_type=F32).astype(BF)
        part = jnp.dot(ret, back_ref[p], preferred_element_type=F32)
        total = part if total is None else total + part
    out_ref[...] = total.T.reshape(8, 2, 16, rows).astype(BF)


def mute(group, samples, cut, spread, inv, fwd, back):
    rows = samples.shape[-1]
    return pl.pallas_call(
        mute_kernel,
        in_specs=[SMEM] + [VMEM] * 6,
        out_specs=VMEM,
        scratch_shapes=[pltpu.VMEM((4, rows, 128), BF)],
        out_shape=jax.ShapeDtypeStruct(samples.shape, BF),
        compiler_params=pltpu.CompilerParams(vmem_limit_bytes=24 * MB),
        cost_estimate=pl.CostEstimate(
            flops=8 * rows * NT * 512, bytes_accessed=4 * MB, transcendentals=0
        ),
        name="mute",
    )(group, samples, cut, spread, inv, fwd, back)


def second_kernel(base, core_ref, ret_ref, own_ref, other_ref, keep_ref, send_ref, lhs_ref):
    rows = own_ref.shape[1]
    even = core_ref[0] == 0

    @pl.when(pl.program_id(0) == 0)
    def _():
        for f in range(2):
            direct = ret_ref[:, f].astype(F32)
            crossed = jnp.concatenate([direct[:, 8:], -direct[:, :8]], 1)
            lhs_ref[f] = jnp.concatenate(
                [direct.reshape(128, rows), crossed.reshape(128, rows)], 1
            ).astype(BF)

    parts = []
    step = 4 * rows
    here = pl.ds(pl.multiple_of((base + pl.program_id(0)) * step, 128), step)
    for k, ref in enumerate((own_ref, other_ref)):
        f = core_ref[0] if k == 0 else 1 - core_ref[0]
        parts.append(
            jnp.dot(
                lhs_ref[f],
                ref[:, :, here].reshape(2 * rows, step),
                preferred_element_type=F32,
            ).reshape(8, 2, 8, step)
        )
    parts = [
        jnp.where(even, parts[f], parts[1 - f])[:, k] for f in range(2) for k in range(2)
    ]
    lane = lax.broadcasted_iota(jnp.int32, (8, 8, 128), 2)
    low, first = lane < 64, (lane // 32) % 2 == 0
    pieces = []
    for v in range(4 * rows // 128):
        a, b, c, d = (x[:, :, v * 128 : (v + 1) * 128] for x in parts)
        a, c = jnp.where(low, a, pltpu.roll(c, 64, 2)), jnp.where(low, pltpu.roll(a, 64, 2), c)
        b, d = jnp.where(low, b, pltpu.roll(d, 64, 2)), jnp.where(low, pltpu.roll(b, 64, 2), d)
        a, b = jnp.where(first, a, pltpu.roll(b, 32, 2)), jnp.where(first, pltpu.roll(a, 96, 2), b)
        c, d = jnp.where(first, c, pltpu.roll(d, 32, 2)), jnp.where(first, pltpu.roll(c, 96, 2), d)
        pieces += [a, b, c, d]
    per = rows // 32
    for j in range(2):
        left = jnp.concatenate(pieces[2 * j * per : (2 * j + 1) * per], 1)
        right = jnp.concatenate(pieces[(2 * j + 1) * per : (2 * j + 2) * per], 1)
        keep_ref[:, j] = jnp.where(even, left, right).astype(BF)
        send_ref[:, j] = jnp.where(even, right, left).astype(BF)


def second_product(core, returned, own, other, part):
    freqs = 2
    _, rows, cols = own.shape
    step = 4 * rows
    packed = rows // 32 * 8
    shape = jax.ShapeDtypeStruct((8, 4, packed, 128), BF)
    spec = pl.BlockSpec((8, 2, packed, 128), lambda k, core: (0, k, 0, 0))
    return pl.pallas_call(
        functools.partial(second_kernel, 2 * part),
        grid_spec=pltpu.PrefetchScalarGridSpec(
            num_scalar_prefetch=1,
            grid=(cols // step // 2,),
            in_specs=[
                pl.BlockSpec((8, freqs, 16, rows), lambda k, core: (0, 0, 0, 0)),
                pl.BlockSpec(memory_space=pltpu.VMEM),
                pl.BlockSpec(memory_space=pltpu.VMEM),
            ],
            out_specs=[spec, spec],
            scratch_shapes=[pltpu.VMEM((2, 128, 2 * rows), BF)],
        ),
        out_shape=[shape, shape],
        compiler_params=pltpu.CompilerParams(vmem_limit_bytes=VL2),
        cost_estimate=pl.CostEstimate(
            flops=4 * rows * cols * 128, bytes_accessed=5 * rows * cols, transcendentals=0
        ),
        name="second_product",
    )(core, returned, own, other)


def merge_kernel(a_ref, b_ref, c_ref, d_ref, out_ref):
    for g in range(8):
        out_ref[g, :4] = (a_ref[g].astype(F32) + b_ref[g].astype(F32)).astype(BF)
        out_ref[g, 4:] = (c_ref[g].astype(F32) + d_ref[g].astype(F32)).astype(BF)


def merge(*parts):
    return pl.pallas_call(
        merge_kernel,
        in_specs=[VMEM] * 4,
        out_specs=VMEM,
        out_shape=jax.ShapeDtypeStruct((8, 8) + parts[0].shape[2:], BF),
        compiler_params=pltpu.CompilerParams(vmem_limit_bytes=8 * MB),
        name="merge",
    )(*parts)


def final_kernel(in_ref, cut_ref, spread_ref, inv_ref, out_ref, wide_ref, slab_ref, sem):
    per = in_ref.shape[2] // 8
    total = in_ref[:, 0].astype(F32)
    for j in range(1, 8):
        total += in_ref[:, j].astype(F32)
    slabs = []
    for k in range(per):
        turned = total[:, k * 8 : (k + 1) * 8].reshape(64, 128).T
        slabs.append(jnp.concatenate([turned[t * 32 : (t + 1) * 32] for t in range(4)], 1))
    turned = jnp.concatenate(slabs, 0).astype(BF)
    wide = jnp.dot(turned, spread_ref[...], preferred_element_type=F32)
    for q in range(4):
        wide_ref[q] = wide[:, q * 128 : (q + 1) * 128].astype(BF)
    edge = cut_ref[...].astype(F32).T

    def out(p):
        return pltpu.make_async_copy(slab_ref.at[p], out_ref.at[p], sem.at[p])

    for p in range(8):
        traces = jnp.dot(wide_ref[p // 2], inv_ref[p % 2], preferred_element_type=F32)
        cut = edge[:, p : p + 1].astype(jnp.int32)
        time = lax.broadcasted_iota(jnp.int32, traces.shape, 1)
        slab_ref[p] = jnp.where(time < cut, traces, 0.0)
        out(p).start()
    for p in range(8):
        out(p).wait()


def final(partials, cut, spread, inv):
    rows = cut.shape[1]
    args = (partials, cut, spread, inv)
    return pl.pallas_call(
        final_kernel,
        in_specs=[VMEM] * 4,
        out_specs=pl.BlockSpec(memory_space=pltpu.HBM),
        scratch_shapes=[
            pltpu.VMEM((4, rows, 128), BF),
            pltpu.VMEM((8, rows, NT), F32),
            pltpu.SemaphoreType.DMA((8,)),
        ],
        out_shape=jax.ShapeDtypeStruct((8, rows, NT), F32),
        compiler_params=pltpu.CompilerParams(vmem_limit_bytes=24 * MB),
        cost_estimate=pl.CostEstimate(
            flops=8 * rows * NT * 256, bytes_accessed=12 * MB, transcendentals=0
        ),
        name="final",
    )(*args)


def on_device(refl, refl_scale, focus, first_mute, second_mute):
    _, freqs, rows, _ = refl.shape
    core = lax.axis_index("c").astype(jnp.int32)[None]
    group = lax.axis_index(FREQ).astype(jnp.int32)[None]
    inv, spread, fwd, back, mixed = (jnp.asarray(a) for a in constants(8 * freqs, 8))

    shares = repeat(focus, 8).reshape(16, rows, 128)
    own = lax.all_to_all(shares, ROWS, 0, 0, tiled=True).reshape(16 * rows, 128)
    decoded = pltpu.with_memory_space_constraint(decode(refl, refl_scale), pltpu.HBM)
    other = lax.ppermute(own, "c", SWAP)
    half, dec_own, dec_other = first_own(core, group, decoded, own)
    focused = first_other(core, dec_other, other, half)
    samples = lax.all_to_all(focused, FREQ, 0, 0, tiled=True)
    spectra = mute(group, samples, first_mute.T, spread, inv, fwd, back)
    returned = lax.all_to_all(spectra, FREQ, 0, 0, tiled=True)
    keep_a, send_a = second_product(core, returned, dec_own, dec_other, 0)
    got_a = lax.ppermute(send_a, "c", SWAP)
    keep_b, send_b = second_product(core, returned, dec_own, dec_other, 1)
    got_b = lax.ppermute(send_b, "c", SWAP)
    summed = merge(keep_a, got_a, keep_b, got_b)
    partials = lax.all_to_all(
        summed.reshape(64, -1, 128), FREQ + ("zh", "x"), 0, 0, tiled=True
    )
    return final(partials.reshape(8, 8, -1, 128), second_mute, mixed, inv)


def solution(mesh):
    fine = Mesh(mesh.devices.reshape(4, 2, 2, 4, 2), ("y", "zl", "zh", "x", "c"))
    in_specs = (
        P(None, FREQ, ROWS, None),
        P(FREQ, ROWS, None),
        P(FREQ, ROWS, None),
        P(ROWS, None),
        P(FREQ, ROWS),
    )
    return jax.shard_map(
        on_device, mesh=fine, in_specs=in_specs, out_specs=P(FREQ, ROWS, None), check_vma=False
    )
```

```python
import functools
import math

import jax
import jax.numpy as jnp
import numpy as np
from jax import lax
from jax.experimental import pallas as pl
from jax.experimental.pallas import tpu as pltpu
from jax.sharding import Mesh
from jax.sharding import PartitionSpec as P

NT = 1024
LOWBIN = 24
FREQ = ("y", "zl")
ROWS = ("zh", "x", "c")
SWAP = ((0, 1), (1, 0))
BF = jnp.bfloat16
F32 = jnp.float32
MB = 1 << 20
VL1 = 20 * MB
VL2 = 26 * MB
KSTEP = 1152
AHEAD = 8


def tables(freq_total):
    phases = (
        (LOWBIN + np.arange(freq_total))[:, None] * np.arange(NT)[None, :] % NT
    ) * (2.0 * math.pi / NT)
    inward = 1.0 / math.sqrt(2.0 * freq_total)
    outward = 2.0 / (NT * inward)
    rows = np.stack([np.cos(phases), -np.sin(phases)], 1).reshape(2 * freq_total, NT)
    return rows * inward, rows * outward


def split(table):
    upper = table.astype(BF)
    lower = (table - upper.astype(np.float64)).astype(BF)
    return upper, lower


def constants(freq_total, group):
    inverse, forward = tables(freq_total)
    rows = 2 * freq_total
    upper, lower = split(inverse)
    pair = np.concatenate([upper, lower], 0)
    zero = np.zeros_like(pair)
    inv = np.stack([np.concatenate([pair, zero], 0), np.concatenate([zero, pair], 0)])
    spread = np.zeros((rows * group, 2 * rows * group), BF)
    for q in range(rows):
        for p in range(group):
            for h in range(2):
                spread[q * group + p, p * 2 * rows + h * rows + q] = 1
    fwd = np.zeros((NT, 128), BF)
    fwd[:, :rows] = forward.T.astype(BF)
    back = np.zeros((group, 128, rows * group), BF)
    for q in range(rows):
        for p in range(group):
            back[p, q, q * group + p] = 1
    mixed = spread.reshape(group, 2, 2, group, -1).transpose(1, 2, 0, 3, 4).reshape(spread.shape)
    return inv, spread, fwd, back, mixed


def repeat_kernel(in_ref, out_ref, sem):
    copies = [
        pltpu.make_async_copy(in_ref, out_ref.at[k], sem.at[k]) for k in range(out_ref.shape[0])
    ]
    for copy in copies:
        copy.start()
    for copy in copies:
        copy.wait()


def repeat(array, times):
    return pl.pallas_call(
        repeat_kernel,
        in_specs=[pl.BlockSpec(memory_space=pltpu.VMEM)],
        out_specs=pl.BlockSpec(memory_space=pltpu.HBM),
        scratch_shapes=[pltpu.SemaphoreType.DMA((times,))],
        out_shape=jax.ShapeDtypeStruct((times,) + array.shape, array.dtype),
        name="repeat",
    )(array)


def decode_kernel(refl_ref, scale_ref, out_ref):
    blocks = scale_ref.shape[-1]
    for b in range(blocks):
        scale = scale_ref[0, :, b : b + 1]
        for k in range(2):
            part = refl_ref[k, 0, :, b * 128 : (b + 1) * 128].astype(F32)
            out_ref[k, 0, :, b * 128 : (b + 1) * 128] = (part * scale).astype(BF)


def decode(refl, scale):
    _, freqs, rows, cols = refl.shape
    step = rows
    return pl.pallas_call(
        decode_kernel,
        grid=(freqs, rows // step),
        in_specs=[
            pl.BlockSpec((2, 1, step, cols), lambda f, s: (0, f, s, 0)),
            pl.BlockSpec((1, step, scale.shape[-1]), lambda f, s: (f, s, 0)),
        ],
        out_specs=pl.BlockSpec((2, 1, step, cols), lambda f, s: (0, f, s, 0)),
        out_shape=jax.ShapeDtypeStruct(refl.shape, BF),
        compiler_params=pltpu.CompilerParams(vmem_limit_bytes=52 * MB),
        cost_estimate=pl.CostEstimate(
            flops=refl.size, bytes_accessed=4 * refl.size, transcendentals=0
        ),
        name="decode",
    )(refl, scale)


def turn(sums, rows):
    direct = sums[:rows]
    crossed = pltpu.roll(sums[rows:], 64, 1)
    lane = lax.broadcasted_iota(jnp.int32, direct.shape, 1)
    both = direct + jnp.where(lane < 64, -crossed, crossed)
    turned = both.T.reshape(2, 8, 8, rows)
    return jnp.concatenate([turned[0], turned[1]], 1).astype(BF)


def first_own_kernel(core_ref, group_ref, dec_ref, focus_ref, out_ref, own_ref, other_ref, acc_ref, sem):
    f = core_ref[0]
    _, rows, cols = own_ref.shape
    spans = [slice(k * KSTEP, (k + 1) * KSTEP) for k in range(cols // KSTEP)]
    copies = []
    for ref, which in ((own_ref, f), (other_ref, 1 - f)):
        for here in spans:
            copies.append(
                pltpu.make_async_copy(
                    dec_ref.at[:, which, :, here], ref.at[:, :, here], sem.at[len(copies)]
                )
            )
    for copy in copies[:AHEAD]:
        copy.start()
    for k, here in enumerate(spans):
        copies[k].wait()
        if k + AHEAD < len(copies):
            copies[k + AHEAD].start()
        part = jnp.dot(
            own_ref[:, :, here].reshape(2 * rows, KSTEP),
            focus_ref[here],
            preferred_element_type=F32,
        )
        if k == 0:
            acc_ref[...] = part
        else:
            acc_ref[...] += part
    for copy in copies[len(spans) + AHEAD :]:
        copy.start()
    out_ref[:, f] = turn(acc_ref[...], rows)
    for copy in copies[len(spans) :]:
        copy.wait()


def first_other_kernel(core_ref, dec_ref, focus_ref, half_ref, out_ref, acc_ref):
    f = 1 - core_ref[0]
    _, rows, cols = dec_ref.shape
    for k in range(cols // KSTEP):
        here = slice(k * KSTEP, (k + 1) * KSTEP)
        part = jnp.dot(
            dec_ref[:, :, here].reshape(2 * rows, KSTEP),
            focus_ref[here],
            preferred_element_type=F32,
        )
        if k == 0:
            acc_ref[...] = part
        else:
            acc_ref[...] += part
    out_ref[:, f] = turn(acc_ref[...], rows)
    out_ref[:, 1 - f] = half_ref[:, 1 - f]


VMEM = pl.BlockSpec(memory_space=pltpu.VMEM)
SMEM = pl.BlockSpec(memory_space=pltpu.SMEM)


def first_own(core, group, decoded, focus):
    _, freqs, rows, cols = decoded.shape
    held = jax.ShapeDtypeStruct((2, rows, cols), BF)
    return pl.pallas_call(
        first_own_kernel,
        in_specs=[SMEM, SMEM, pl.BlockSpec(memory_space=pltpu.HBM), VMEM],
        out_specs=[VMEM] * 3,
        scratch_shapes=[
            pltpu.VMEM((2 * rows, 128), F32),
            pltpu.SemaphoreType.DMA((2 * cols // KSTEP,)),
        ],
        out_shape=[jax.ShapeDtypeStruct((8, freqs, 16, rows), BF), held, held],
        compiler_params=pltpu.CompilerParams(vmem_limit_bytes=VL1),
        cost_estimate=pl.CostEstimate(
            flops=4 * rows * cols * 128, bytes_accessed=8 * rows * cols, transcendentals=0
        ),
        name="first_own",
    )(core, group, decoded, focus)


def first_other(core, held, focus, half):
    _, rows, cols = held.shape
    return pl.pallas_call(
        first_other_kernel,
        in_specs=[SMEM, VMEM, VMEM, VMEM],
        out_specs=VMEM,
        scratch_shapes=[pltpu.VMEM((2 * rows, 128), F32)],
        out_shape=jax.ShapeDtypeStruct(half.shape, BF),
        compiler_params=pltpu.CompilerParams(vmem_limit_bytes=VL1),
        cost_estimate=pl.CostEstimate(
            flops=4 * rows * cols * 128, bytes_accessed=4 * rows * cols, transcendentals=0
        ),
        name="first_other",
    )(core, held, focus, half)


def mute_kernel(group_ref, in_ref, cut_ref, spread_ref, inv_ref, fwd_ref, back_ref, out_ref, wide_ref):
    rows = in_ref.shape[-1]
    turned = in_ref[...].reshape(256, rows).astype(F32).T.astype(BF)
    wide = jnp.dot(turned, spread_ref[...], preferred_element_type=F32)
    for q in range(4):
        wide_ref[q] = wide[:, q * 128 : (q + 1) * 128].astype(BF)
    own = pl.ds(pl.multiple_of(group_ref[0] * 8, 8), 8)
    edge = cut_ref[own].astype(F32).T
    total = None
    for p in range(8):
        traces = jnp.dot(wide_ref[p // 2], inv_ref[p % 2], preferred_element_type=F32)
        cut = edge[:, p : p + 1].astype(jnp.int32)
        time = lax.broadcasted_iota(jnp.int32, traces.shape, 1)
        kept = jnp.where(time < cut, traces, 0.0).astype(BF)
        ret = jnp.dot(kept, fwd_ref[...], preferred_element_type=F32).astype(BF)
        part = jnp.dot(ret, back_ref[p], preferred_element_type=F32)
        total = part if total is None else total + part
    out_ref[...] = total.T.reshape(8, 2, 16, rows).astype(BF)


def mute(group, samples, cut, spread, inv, fwd, back):
    rows = samples.shape[-1]
    return pl.pallas_call(
        mute_kernel,
        in_specs=[SMEM] + [VMEM] * 6,
        out_specs=VMEM,
        scratch_shapes=[pltpu.VMEM((4, rows, 128), BF)],
        out_shape=jax.ShapeDtypeStruct(samples.shape, BF),
        compiler_params=pltpu.CompilerParams(vmem_limit_bytes=24 * MB),
        cost_estimate=pl.CostEstimate(
            flops=8 * rows * NT * 512, bytes_accessed=4 * MB, transcendentals=0
        ),
        name="mute",
    )(group, samples, cut, spread, inv, fwd, back)


def second_kernel(base, core_ref, ret_ref, own_ref, other_ref, keep_ref, send_ref, lhs_ref):
    rows = own_ref.shape[1]
    even = core_ref[0] == 0

    @pl.when(pl.program_id(0) == 0)
    def _():
        for f in range(2):
            direct = ret_ref[:, f].astype(F32)
            crossed = jnp.concatenate([direct[:, 8:], -direct[:, :8]], 1)
            lhs_ref[f] = jnp.concatenate(
                [direct.reshape(128, rows), crossed.reshape(128, rows)], 1
            ).astype(BF)

    parts = []
    step = 4 * rows
    here = pl.ds(pl.multiple_of((base + pl.program_id(0)) * step, 128), step)
    for k, ref in enumerate((own_ref, other_ref)):
        f = core_ref[0] if k == 0 else 1 - core_ref[0]
        parts.append(
            jnp.dot(
                lhs_ref[f],
                ref[:, :, here].reshape(2 * rows, step),
                preferred_element_type=F32,
            ).reshape(8, 2, 8, step)
        )
    parts = [
        jnp.where(even, parts[f], parts[1 - f])[:, k] for f in range(2) for k in range(2)
    ]
    lane = lax.broadcasted_iota(jnp.int32, (8, 8, 128), 2)
    low, first = lane < 64, (lane // 32) % 2 == 0
    pieces = []
    for v in range(4 * rows // 128):
        a, b, c, d = (x[:, :, v * 128 : (v + 1) * 128] for x in parts)
        a, c = jnp.where(low, a, pltpu.roll(c, 64, 2)), jnp.where(low, pltpu.roll(a, 64, 2), c)
        b, d = jnp.where(low, b, pltpu.roll(d, 64, 2)), jnp.where(low, pltpu.roll(b, 64, 2), d)
        a, b = jnp.where(first, a, pltpu.roll(b, 32, 2)), jnp.where(first, pltpu.roll(a, 96, 2), b)
        c, d = jnp.where(first, c, pltpu.roll(d, 32, 2)), jnp.where(first, pltpu.roll(c, 96, 2), d)
        pieces += [a, b, c, d]
    per = rows // 32
    for j in range(2):
        left = jnp.concatenate(pieces[2 * j * per : (2 * j + 1) * per], 1)
        right = jnp.concatenate(pieces[(2 * j + 1) * per : (2 * j + 2) * per], 1)
        keep_ref[:, j] = jnp.where(even, left, right).astype(BF)
        send_ref[:, j] = jnp.where(even, right, left).astype(BF)


def second_product(core, returned, own, other, part):
    freqs = 2
    _, rows, cols = own.shape
    step = 4 * rows
    packed = rows // 32 * 8
    shape = jax.ShapeDtypeStruct((8, 4, packed, 128), BF)
    spec = pl.BlockSpec((8, 2, packed, 128), lambda k, core: (0, k, 0, 0))
    return pl.pallas_call(
        functools.partial(second_kernel, 2 * part),
        grid_spec=pltpu.PrefetchScalarGridSpec(
            num_scalar_prefetch=1,
            grid=(cols // step // 2,),
            in_specs=[
                pl.BlockSpec((8, freqs, 16, rows), lambda k, core: (0, 0, 0, 0)),
                pl.BlockSpec(memory_space=pltpu.VMEM),
                pl.BlockSpec(memory_space=pltpu.VMEM),
            ],
            out_specs=[spec, spec],
            scratch_shapes=[pltpu.VMEM((2, 128, 2 * rows), BF)],
        ),
        out_shape=[shape, shape],
        compiler_params=pltpu.CompilerParams(vmem_limit_bytes=VL2),
        cost_estimate=pl.CostEstimate(
            flops=4 * rows * cols * 128, bytes_accessed=5 * rows * cols, transcendentals=0
        ),
        name="second_product",
    )(core, returned, own, other)


def merge_kernel(a_ref, b_ref, c_ref, d_ref, out_ref):
    for g in range(8):
        out_ref[g, :4] = (a_ref[g].astype(F32) + b_ref[g].astype(F32)).astype(BF)
        out_ref[g, 4:] = (c_ref[g].astype(F32) + d_ref[g].astype(F32)).astype(BF)


def merge(*parts):
    return pl.pallas_call(
        merge_kernel,
        in_specs=[VMEM] * 4,
        out_specs=VMEM,
        out_shape=jax.ShapeDtypeStruct((8, 8) + parts[0].shape[2:], BF),
        compiler_params=pltpu.CompilerParams(vmem_limit_bytes=8 * MB),
        name="merge",
    )(*parts)


def final_kernel(in_ref, cut_ref, spread_ref, inv_ref, out_ref, wide_ref, slab_ref, sem):
    per = in_ref.shape[2] // 8
    rows = cut_ref.shape[1]
    total = in_ref[:, 0].astype(F32)
    for j in range(1, 8):
        total += in_ref[:, j].astype(F32)
    slabs = []
    for k in range(per):
        turned = total[:, k * 8 : (k + 1) * 8].reshape(64, 128).T
        slabs.append(jnp.concatenate([turned[t * 32 : (t + 1) * 32] for t in range(4)], 1))
    turned = jnp.concatenate(slabs, 0).astype(BF)
    wide = jnp.dot(turned, spread_ref[...], preferred_element_type=F32)
    for q in range(4):
        wide_ref[q] = wide[:, q * 128 : (q + 1) * 128].astype(BF)
    edge = cut_ref[...].astype(F32).T

    third = rows // 3

    def out(p):
        return [
            pltpu.make_async_copy(
                slab_ref.at[p, h * third : (h + 1) * third],
                out_ref.at[p, h * third : (h + 1) * third],
                sem.at[p, h],
            )
            for h in range(3)
        ]

    for p in range(8):
        traces = jnp.dot(wide_ref[p // 2], inv_ref[p % 2], preferred_element_type=F32)
        cut = edge[:, p : p + 1].astype(jnp.int32)
        time = lax.broadcasted_iota(jnp.int32, traces.shape, 1)
        slab_ref[p] = jnp.where(time < cut, traces, 0.0)
        for copy in out(p):
            copy.start()
    for p in range(8):
        for copy in out(p):
            copy.wait()


def final(partials, cut, spread, inv):
    rows = cut.shape[1]
    args = (partials, cut, spread, inv)
    return pl.pallas_call(
        final_kernel,
        in_specs=[VMEM] * 4,
        out_specs=pl.BlockSpec(memory_space=pltpu.HBM),
        scratch_shapes=[
            pltpu.VMEM((4, rows, 128), BF),
            pltpu.VMEM((8, rows, NT), F32),
            pltpu.SemaphoreType.DMA((8, 3)),
        ],
        out_shape=jax.ShapeDtypeStruct((8, rows, NT), F32),
        compiler_params=pltpu.CompilerParams(vmem_limit_bytes=24 * MB),
        cost_estimate=pl.CostEstimate(
            flops=8 * rows * NT * 256, bytes_accessed=12 * MB, transcendentals=0
        ),
        name="final",
    )(*args)


def on_device(refl, refl_scale, focus, first_mute, second_mute):
    _, freqs, rows, _ = refl.shape
    core = lax.axis_index("c").astype(jnp.int32)[None]
    group = lax.axis_index(FREQ).astype(jnp.int32)[None]
    inv, spread, fwd, back, mixed = (jnp.asarray(a) for a in constants(8 * freqs, 8))

    shares = repeat(focus, 8).reshape(16, rows, 128)
    own = lax.all_to_all(shares, ROWS, 0, 0, tiled=True).reshape(16 * rows, 128)
    decoded = pltpu.with_memory_space_constraint(decode(refl, refl_scale), pltpu.HBM)
    other = lax.ppermute(own, "c", SWAP)
    half, dec_own, dec_other = first_own(core, group, decoded, own)
    focused = first_other(core, dec_other, other, half)
    samples = lax.all_to_all(focused, FREQ, 0, 0, tiled=True)
    spectra = mute(group, samples, first_mute.T, spread, inv, fwd, back)
    returned = lax.all_to_all(spectra, FREQ, 0, 0, tiled=True)
    keep_a, send_a = second_product(core, returned, dec_own, dec_other, 0)
    got_a = lax.ppermute(send_a, "c", SWAP)
    keep_b, send_b = second_product(core, returned, dec_own, dec_other, 1)
    got_b = lax.ppermute(send_b, "c", SWAP)
    summed = merge(keep_a, got_a, keep_b, got_b)
    partials = lax.all_to_all(
        summed.reshape(64, -1, 128), FREQ + ("zh", "x"), 0, 0, tiled=True
    )
    return final(partials.reshape(8, 8, -1, 128), second_mute, mixed, inv)


def solution(mesh):
    fine = Mesh(mesh.devices.reshape(4, 2, 2, 4, 2), ("y", "zl", "zh", "x", "c"))
    in_specs = (
        P(None, FREQ, ROWS, None),
        P(FREQ, ROWS, None),
        P(FREQ, ROWS, None),
        P(ROWS, None),
        P(FREQ, ROWS),
    )
    return jax.shard_map(
        on_device, mesh=fine, in_specs=in_specs, out_specs=P(FREQ, ROWS, None), check_vma=False
    )
```
